32 devices in a mesh: dev: 32 (over z, y, x, core).
Axes of the slice: x: 2, y: 2, z: 4, core: 2. Of those that a mesh axis runs over, the one named last changes fastest.
Arguments:
- layer_input: bfloat16 [5120, 1024], P('dev'), may hold values from -6 to 6
- ln1_gain: bfloat16 [1024], P('dev'), may hold values from 0.5 to 1.5
- ln1_bias: bfloat16 [1024], P('dev'), may hold values from -3 to 3
- qkv_weight: bfloat16 [1024, 3072], P('dev'), may hold values from -1.40625 to 1.40625
- qkv_bias: bfloat16 [3072], P('dev'), may hold values from -3 to 3
- dense_weight: bfloat16 [1024, 1024], P('dev'), may hold values from -0.75 to 0.75
- dense_bias: bfloat16 [1024], P('dev'), may hold values from -3 to 3
- ln2_gain: bfloat16 [1024], P('dev'), may hold values from 0.5 to 1.5
- ln2_bias: bfloat16 [1024], P('dev'), may hold values from -3 to 3
- fc_in_weight: bfloat16 [1024, 4096], P('dev'), may hold values from -0.1875 to 0.1875
- fc_in_bias: bfloat16 [4096], P('dev'), may hold values from -3 to 3
- fc_out_weight: bfloat16 [4096, 1024], P('dev'), may hold values from -0.09375 to 0.09375
- fc_out_bias: bfloat16 [1024], P('dev'), may hold values from -3 to 3
- positions: int32 [5120], P('dev'), may hold values from 0 to 511, as said below
- cotangent: bfloat16 [5120, 1024], P('dev'), may hold values from -6 to 6
Outputs:
- output: bfloat16 [5120, 1024], P('dev')
- grad_input: float32 [5120, 1024], P('dev')
- grad_ln1_gain: float32 [1024], P('dev')
- grad_ln1_bias: float32 [1024], P('dev')
- grad_qkv_weight: float32 [1024, 3072], P('dev')
- grad_qkv_bias: float32 [3072], P('dev')
- grad_dense_weight: float32 [1024, 1024], P('dev')
- grad_dense_bias: float32 [1024], P('dev')
- grad_ln2_gain: float32 [1024], P('dev')
- grad_ln2_bias: float32 [1024], P('dev')
- grad_fc_in_weight: float32 [1024, 4096], P('dev')
- grad_fc_in_bias: float32 [4096], P('dev')
- grad_fc_out_weight: float32 [4096, 1024], P('dev')
- grad_fc_out_bias: float32 [1024], P('dev')
The draws below stay inside these ranges and needn't reach their ends.
Inputs may be any that keep to these rules, and one draw needn't show every extreme that they name: `positions`: documents lie end to end over all tokens; a token of position p has the p tokens before it in its document, and a token of position 0 starts a document; no document is longer than 512 tokens, and in every draw one document has exactly 512 tokens.
All inputs are finite; a program needn't handle non-finite values.
Results may differ from the reference program's by a relative error of at most 0.0095.
Values may be sent and summed in bfloat16 or wider, within the bound.
A program may use at most 256 MiB of HBM per device.

```python
import jax
import jax.numpy as jnp
from jax import lax

D = 1024
HEADS = 16
HD = 64
ROT = 16
FF = 4096
SEQ = 512
TOKENS = 5120


def draw_positions(key, part):
    own_key = jax.random.fold_in(key, 11)
    token_index = jnp.arange(TOKENS, dtype=jnp.int32)
    column = token_index % SEQ
    first_key, second_key = jax.random.split(own_key)
    coin_marks = jax.random.randint(first_key, (TOKENS,), 0, max(SEQ // 4, 2))
    offset = jax.random.randint(second_key, (), SEQ // 4, 3 * SEQ // 4 + 1)
    long_start = TOKENS // 2 - offset
    inside = (token_index > long_start) & (token_index < long_start + SEQ)
    starts = ((column == 0) | (coin_marks == 0) | (token_index == long_start) | (token_index == long_start + SEQ)) & jnp.logical_not(inside)
    doc_begin = lax.cummax(jnp.where(starts, token_index, 0), axis=0)
    return (token_index - doc_begin).astype(jnp.int32)


def draw_qkv_weight(key, part):
    own_key = jax.random.fold_in(key, 3)
    std_scale = D ** (-0.5)
    base_draw = jnp.clip(jax.random.normal(own_key, (D, 3 * D), jnp.float32), -6.0, 6.0)
    return (base_draw * std_scale).astype(jnp.bfloat16)


def raised(values, rng, source, target, shards_of, factor):
    owner, partner = [(jnp.arange(values.shape[axis_at]) // (values.shape[axis_at] // shards_of)).reshape([-1 if axis == axis_at else 1 for axis in range(values.ndim)]) for axis_at in (source, target)]
    chosen = jax.random.permutation(rng, shards_of)[partner]
    strong = (owner == chosen) | (owner == (partner + shards_of // 2) % shards_of)
    return jnp.where(strong, factor * values, values)


def shard_levels(rng, shape, shards, least, top_value):
    def one(dim, parts):
        heights = jax.random.uniform(jax.random.fold_in(jax.random.fold_in(rng, 6), dim), (parts,), jnp.float32, least / len(shards), top_value / len(shards))
        return jnp.repeat(jnp.exp(heights), shape[dim] // parts).reshape((-1,) + (1,) * (len(shape) - dim - 1))

    level = one(*shards[0])
    for cut in shards[1:]:
        level = level * one(*cut)
    return level


def noise(key, dims, scale, most, cuts=(), kind=jnp.bfloat16):
    values = scale * jax.random.normal(key, dims, jnp.float32)
    if cuts:
        values = values * shard_levels(key, dims, cuts, -0.22, 0.18)
    return jnp.clip(values, -most, most).astype(kind)


def gaussian_with(key, shape, scale, limit, cuts, heavy, held_as=jnp.bfloat16):
    entries = scale * jax.random.normal(key, shape, jnp.float32)
    if cuts:
        entries = entries * shard_levels(key, shape, cuts, -0.22, 0.18)
    return jnp.clip(raised(entries, jax.random.fold_in(key, 3), *heavy), -limit, limit).astype(held_as)


def setup_inputs(seed: int = 0) -> dict:
    key_of = jax.random.split(jax.random.key(seed), 16)
    layer_input = gaussian_with(key_of[0], (TOKENS, D), 1.0, 6.0, ((0, 32),), (0, 1, 32, 2.75))
    ln1_gain = jnp.clip(1.0 + 0.1 * jax.random.normal(key_of[1], (D,), jnp.float32), 0.5, 1.5).astype(jnp.bfloat16)
    ln1_bias = noise(key_of[2], (D,), 0.5, 3.0, ((0, 32),))
    qkv_weight = draw_qkv_weight(jax.random.fold_in(key_of[15], 71), 0)
    qkv_bias = noise(key_of[4], (3 * D,), 0.5, 3.0, ((0, 32),))
    dense_weight = noise(key_of[5], (D, D), (D // 16) ** -0.5, 0.75, ((0, 32),))
    dense_bias = noise(key_of[6], (D,), 0.5, 3.0, ((0, 32),))
    ln2_gain = jnp.clip(1.0 + 0.1 * jax.random.normal(key_of[7], (D,), jnp.float32), 0.5, 1.5).astype(jnp.bfloat16)
    ln2_bias = noise(key_of[8], (D,), 0.5, 3.0, ((0, 32),))
    fc_in_weight = noise(key_of[9], (D, FF), D ** -0.5, 0.1875, ((0, 32),))
    fc_in_bias = noise(key_of[10], (FF,), 0.5, 3.0, ((0, 32),))
    fc_out_weight = noise(key_of[11], (FF, D), FF ** -0.5, 0.09375, ((0, 32),))
    fc_out_bias = noise(key_of[12], (D,), 0.5, 3.0, ((0, 32),))
    positions = draw_positions(jax.random.fold_in(key_of[15], 71), 0)
    cotangent = gaussian_with(key_of[14], (TOKENS, D), 1.0, 6.0, ((0, 32),), (0, 1, 32, 2.75))
    return dict(layer_input=layer_input, ln1_gain=ln1_gain, ln1_bias=ln1_bias, qkv_weight=qkv_weight, qkv_bias=qkv_bias, dense_weight=dense_weight, dense_bias=dense_bias, ln2_gain=ln2_gain, ln2_bias=ln2_bias, fc_in_weight=fc_in_weight, fc_in_bias=fc_in_bias, fc_out_weight=fc_out_weight, fc_out_bias=fc_out_bias, positions=positions, cotangent=cotangent)


EPSILON = 1e-05
ROPE_BASE = 10000.0

def norm_stats(inputs):
    values_f = inputs.astype(jnp.float32)
    centre = lax.optimization_barrier(jnp.mean(values_f, axis=-1, keepdims=True))
    shifted = values_f - centre
    variance = lax.optimization_barrier(jnp.mean(shifted * shifted, axis=-1, keepdims=True))
    inv_scale = lax.rsqrt(variance + EPSILON)
    return (shifted * inv_scale, inv_scale)

def rotary_tables(positions, rot_half):
    counter = jnp.arange(rot_half).astype(jnp.float32)
    frequency = ROPE_BASE ** (-2.0 * counter / (2.0 * rot_half))
    angles = positions.astype(jnp.float32)[:, None] * frequency[None, :]
    return (jnp.cos(angles), jnp.sin(angles))

def rotate(head_rows, cos_table, sin_table, orient):
    halfway = cos_table.shape[-1]
    leading = head_rows[..., :halfway]
    trailing = head_rows[..., halfway:2 * halfway]
    remainder = head_rows[..., 2 * halfway:]
    cosine = cos_table[:, None, :]
    sine_part = orient * sin_table[:, None, :]
    return jnp.concatenate([leading * cosine - trailing * sine_part, trailing * cosine + leading * sine_part, remainder], axis=-1)

def gelu_pair(pre_act):
    cumulative = 0.5 * (1.0 + lax.erf(pre_act * 0.7071067811865476))
    density = jnp.exp(-0.5 * pre_act * pre_act) * 0.3989422804014327
    return (pre_act * cumulative, cumulative + pre_act * density)

def row_sum_product(left_side, right_side):
    return lax.dot_general(left_side, right_side, (((0,), (0,)), ((), ())), preferred_element_type=jnp.float32)

def times_transpose(left_side, right_side):
    return lax.dot_general(left_side, right_side, (((1,), (1,)), ((), ())), preferred_element_type=jnp.float32)

def masked_scores(queries, keys_rot, allowed):
    scores = jnp.einsum('qhd,khd->hqk', queries.astype(jnp.float32), keys_rot.astype(jnp.float32)) * HD ** (-0.5)
    return jnp.where(allowed[None], scores, -jnp.inf)

def attend(queries, keys_rot, values_v, allowed):
    scores = masked_scores(queries, keys_rot, allowed)
    row_max = lax.optimization_barrier(jnp.max(scores, axis=-1, keepdims=True))
    exp_total = lax.optimization_barrier(jnp.sum(jnp.exp(scores - row_max), axis=-1, keepdims=True))
    log_total = row_max + jnp.log(exp_total)
    probs_b = jnp.exp(scores - log_total).astype(jnp.bfloat16)
    context = jnp.einsum('hqk,khd->qhd', probs_b.astype(jnp.float32), values_v.astype(jnp.float32))
    return (context, log_total)

def attend_back(queries, keys_rot, values_v, allowed, log_total, grad_context):
    scores = masked_scores(queries, keys_rot, allowed)
    probs = jnp.exp(scores - log_total)
    probs_b = probs.astype(jnp.bfloat16)
    grad_probs = jnp.einsum('qhd,khd->hqk', grad_context.astype(jnp.float32), values_v.astype(jnp.float32))
    row_dot = lax.optimization_barrier(jnp.sum(probs * grad_probs, axis=-1, keepdims=True))
    grad_scores = (probs * (grad_probs - row_dot) * HD ** (-0.5)).astype(jnp.bfloat16)
    grad_queries = jnp.einsum('hqk,khd->qhd', grad_scores.astype(jnp.float32), keys_rot.astype(jnp.float32))
    grad_keys = jnp.einsum('hqk,qhd->khd', grad_scores.astype(jnp.float32), queries.astype(jnp.float32))
    grad_values = jnp.einsum('hqk,qhd->khd', probs_b.astype(jnp.float32), grad_context.astype(jnp.float32))
    return (grad_queries, grad_keys, grad_values)

def reference(layer_input, ln1_gain, ln1_bias, qkv_weight, qkv_bias, dense_weight, dense_bias, ln2_gain, ln2_bias, fc_in_weight, fc_in_bias, fc_out_weight, fc_out_bias, positions, cotangent):
    num_seqs = layer_input.shape[0] // SEQ
    gain_one = ln1_gain.astype(jnp.float32)
    shift_one = ln1_bias.astype(jnp.float32)
    gain_two = ln2_gain.astype(jnp.float32)
    shift_two = ln2_bias.astype(jnp.float32)
    bias_qkv = qkv_bias.astype(jnp.float32)
    bias_dense = dense_bias.astype(jnp.float32)
    bias_in = fc_in_bias.astype(jnp.float32)
    bias_out = fc_out_bias.astype(jnp.float32)
    input_blocks = layer_input.reshape(num_seqs, SEQ, D)
    place_blocks = positions.reshape(num_seqs, SEQ)
    top_blocks = cotangent.reshape(num_seqs, SEQ, D)

    def project(item):
        tokens_in, place = item
        normed, inv_scale = norm_stats(tokens_in)
        left_attn = (normed * gain_one + shift_one).astype(jnp.bfloat16)
        mixed_qkv = jnp.dot(left_attn, qkv_weight, preferred_element_type=jnp.float32) + bias_qkv
        cos_table, sin_table = rotary_tables(place, ROT // 2)
        queries = rotate(mixed_qkv[:, :D].reshape(SEQ, HEADS, HD), cos_table, sin_table, 1.0).astype(jnp.bfloat16)
        keys_rot = rotate(mixed_qkv[:, D:2 * D].reshape(SEQ, HEADS, HD), cos_table, sin_table, 1.0).astype(jnp.bfloat16)
        values_v = mixed_qkv[:, 2 * D:].reshape(SEQ, HEADS, HD).astype(jnp.bfloat16)
        return (queries, keys_rot, values_v)
    all_queries, all_keys, all_values = lax.map(project, (input_blocks, place_blocks))
    empty_block = jnp.zeros((1, SEQ, HEADS, HD), jnp.bfloat16)
    prev_keys = jnp.concatenate([empty_block, all_keys[:-1]], axis=0)
    prev_values = jnp.concatenate([empty_block, all_values[:-1]], axis=0)

    def attention_block(item):
        queries, keys_before, keys_now, values_before, values_now, place, grad_top = item
        win_keys = jnp.concatenate([keys_before, keys_now], axis=0)
        win_values = jnp.concatenate([values_before, values_now], axis=0)
        query_index = jnp.arange(SEQ, dtype=jnp.int32) + SEQ
        key_index = jnp.arange(2 * SEQ, dtype=jnp.int32)
        spread = query_index[:, None] - key_index[None, :]
        allowed = (spread >= 0) & (spread <= place[:, None])
        context, log_total = attend(queries, win_keys, win_values, allowed)
        context_b = context.reshape(SEQ, D).astype(jnp.bfloat16)
        grad_context = times_transpose(grad_top, dense_weight).astype(jnp.bfloat16).reshape(SEQ, HEADS, HD)
        g_queries, g_keys, g_values = attend_back(queries, win_keys, win_values, allowed, log_total, grad_context)
        return (context_b, g_queries, g_keys, g_values)
    all_context, all_gq, win_gk, win_gv = lax.map(attention_block, (all_queries, prev_keys, all_keys, prev_values, all_values, place_blocks, top_blocks))
    empty_grad = jnp.zeros((1, SEQ, HEADS, HD), jnp.float32)
    own_gk = win_gk[:, SEQ:] + jnp.concatenate([win_gk[1:, :SEQ], empty_grad], axis=0)
    own_gv = win_gv[:, SEQ:] + jnp.concatenate([win_gv[1:, :SEQ], empty_grad], axis=0)

    def one_block(totals, seq_item):
        tokens_in, place, grad_top, context_b, g_queries, g_keys, g_values = seq_item
        normed, inv_scale = norm_stats(tokens_in)
        left_attn = (normed * gain_one + shift_one).astype(jnp.bfloat16)
        left_mlp = (normed * gain_two + shift_two).astype(jnp.bfloat16)
        cos_table, sin_table = rotary_tables(place, ROT // 2)
        attn_out = jnp.dot(context_b, dense_weight, preferred_element_type=jnp.float32) + bias_dense
        pre_act = jnp.dot(left_mlp, fc_in_weight, preferred_element_type=jnp.float32) + bias_in
        activated, gelu_slope = gelu_pair(pre_act)
        activated_b = activated.astype(jnp.bfloat16)
        mlp_out = jnp.dot(activated_b, fc_out_weight, preferred_element_type=jnp.float32) + bias_out
        result = (tokens_in.astype(jnp.float32) + attn_out + mlp_out).astype(jnp.bfloat16)
        top_f = grad_top.astype(jnp.float32)
        g_dense_w = row_sum_product(context_b, grad_top)
        g_dense_b = lax.optimization_barrier(jnp.sum(top_f, axis=0))
        g_out_w = row_sum_product(activated_b, grad_top)
        g_out_b = lax.optimization_barrier(jnp.sum(top_f, axis=0))
        grad_pre = times_transpose(grad_top, fc_out_weight) * gelu_slope
        grad_pre_b = grad_pre.astype(jnp.bfloat16)
        g_in_w = row_sum_product(left_mlp, grad_pre_b)
        g_in_b = lax.optimization_barrier(jnp.sum(grad_pre, axis=0))
        grad_left_mlp = times_transpose(grad_pre_b, fc_in_weight)
        back_queries = rotate(g_queries, cos_table, sin_table, -1.0)
        back_keys = rotate(g_keys, cos_table, sin_table, -1.0)
        grad_qkv = jnp.concatenate([back_queries.reshape(SEQ, D), back_keys.reshape(SEQ, D), g_values.reshape(SEQ, D)], axis=1)
        grad_qkv_b = grad_qkv.astype(jnp.bfloat16)
        g_qkv_w = row_sum_product(left_attn, grad_qkv_b)
        g_qkv_b = lax.optimization_barrier(jnp.sum(grad_qkv, axis=0))
        grad_left_attn = times_transpose(grad_qkv_b, qkv_weight)
        g_gain_one = lax.optimization_barrier(jnp.sum(grad_left_attn * normed, axis=0))
        g_shift_one = lax.optimization_barrier(jnp.sum(grad_left_attn, axis=0))
        g_gain_two = lax.optimization_barrier(jnp.sum(grad_left_mlp * normed, axis=0))
        g_shift_two = lax.optimization_barrier(jnp.sum(grad_left_mlp, axis=0))
        grad_normed = grad_left_attn * gain_one + grad_left_mlp * gain_two
        grad_in = top_f + inv_scale * (grad_normed - lax.optimization_barrier(jnp.mean(grad_normed, axis=-1, keepdims=True)) - normed * lax.optimization_barrier(jnp.mean(grad_normed * normed, axis=-1, keepdims=True)))
        terms = (g_gain_one, g_shift_one, g_qkv_w, g_qkv_b, g_dense_w, g_dense_b, g_gain_two, g_shift_two, g_in_w, g_in_b, g_out_w, g_out_b)
        totals = jax.tree.map(jnp.add, totals, terms)
        return (totals, (result, grad_in))
    zero_totals = (jnp.zeros((D,), jnp.float32), jnp.zeros((D,), jnp.float32), jnp.zeros((D, 3 * D), jnp.float32), jnp.zeros((3 * D,), jnp.float32), jnp.zeros((D, D), jnp.float32), jnp.zeros((D,), jnp.float32), jnp.zeros((D,), jnp.float32), jnp.zeros((D,), jnp.float32), jnp.zeros((D, FF), jnp.float32), jnp.zeros((FF,), jnp.float32), jnp.zeros((FF, D), jnp.float32), jnp.zeros((D,), jnp.float32))
    seq_items = (input_blocks, place_blocks, top_blocks, all_context, all_gq, own_gk, own_gv)
    totals, stacked = lax.scan(one_block, zero_totals, seq_items)
    outputs = stacked[0].reshape(num_seqs * SEQ, D)
    grad_in = stacked[1].reshape(num_seqs * SEQ, D)
    return (outputs, grad_in, totals[0], totals[1], totals[2], totals[3], totals[4], totals[5], totals[6], totals[7], totals[8], totals[9], totals[10], totals[11])
```

```python
import jax
import jax.numpy as jnp
from jax import lax
from jax.sharding import Mesh
from jax.sharding import PartitionSpec as P

HEADS = 16
HD = 64
ROT = 16
REACH = 512
GROUP = 8
BLOCK = 256


EPSILON = 1e-05
ROPE_BASE = 10000.0


def norm_stats(inputs):
    values_f = inputs.astype(jnp.float32)
    centre = jnp.mean(values_f, axis=-1, keepdims=True)
    shifted = values_f - centre
    variance = jnp.mean(shifted * shifted, axis=-1, keepdims=True)
    inv_scale = lax.rsqrt(variance + EPSILON)
    return (shifted * inv_scale, inv_scale)


def rotary_tables(positions, lanes):
    place = jnp.arange(lanes, dtype=jnp.int32) % HD
    counter = (place % (ROT // 2)).astype(jnp.float32)
    frequency = ROPE_BASE ** (-2.0 * counter / ROT)
    frequency = jnp.where(place < ROT, frequency, 0.0)
    angles = positions.astype(jnp.float32)[:, None] * frequency[None, :]
    sine = jnp.sin(angles)
    lower = jnp.where(place < ROT // 2, -sine, 0.0)
    upper = jnp.where(place >= ROT // 2, sine, 0.0)
    return (jnp.cos(angles), lower, upper)


def rotate(rows, tables, orient):
    cosine, lower, upper = tables
    ahead = jnp.roll(rows, -(ROT // 2), axis=1)
    behind = jnp.roll(rows, ROT // 2, axis=1)
    return rows * cosine + orient * (ahead * lower + behind * upper)


def windows(rows, blocks, size, span):
    heads = rows.shape[1] // HD
    cut = jnp.stack([rows[i * size : i * size + span] for i in range(blocks)])
    return cut.reshape(blocks, span, heads, HD).transpose(0, 2, 1, 3)


def unwindow(grads, blocks, size, span):
    parts = span // size
    heads = grads.shape[1]
    rows = grads.transpose(0, 2, 1, 3).reshape(blocks, parts, size, heads * HD)
    total = None
    for part in range(parts):
        piece = jnp.pad(rows[:, part], ((part, parts - 1 - part), (0, 0), (0, 0)))
        total = piece if total is None else total + piece
    return total.reshape((blocks + parts - 1) * size, heads * HD)


def gelu_pair(pre_act):
    cumulative = 0.5 * (1.0 + lax.erf(pre_act * 0.7071067811865476))
    density = jnp.exp(-0.5 * pre_act * pre_act) * 0.3989422804014327
    return (pre_act * cumulative, cumulative + pre_act * density)


def row_sum_product(left_side, right_side):
    return lax.dot_general(
        left_side, right_side, (((0,), (0,)), ((), ())), preferred_element_type=jnp.float32
    )


def times_transpose(left_side, right_side):
    return lax.dot_general(
        left_side, right_side, (((1,), (1,)), ((), ())), preferred_element_type=jnp.float32
    )


def body(
    layer_input,
    ln1_gain,
    ln1_bias,
    qkv_weight,
    qkv_bias,
    dense_weight,
    dense_bias,
    ln2_gain,
    ln2_bias,
    fc_in_weight,
    fc_in_bias,
    fc_out_weight,
    fc_out_bias,
    positions,
    cotangent,
):
    bf = jnp.bfloat16
    f32 = jnp.float32
    outer = lax.axis_size("g")
    inner = lax.axis_size("r")
    count = outer * inner
    rank = lax.axis_index("r")
    tok_rows, width = layer_input.shape
    part_rows = qkv_weight.shape[0]
    share = width // inner
    unit = fc_out_weight.shape[0]
    hidden = outer * unit
    rows = inner * tok_rows

    place = jnp.stack([positions // 256, positions % 256], axis=1).astype(bf)
    place = jnp.pad(place, ((0, 0), (0, 126)))
    tokens = jnp.concatenate([layer_input, cotangent, place], axis=1)
    tokens = lax.all_gather(tokens, "r", axis=0, tiled=True)
    group_in = tokens[:, :width]
    group_top = tokens[:, width : 2 * width]
    place = tokens[:, 2 * width : 2 * width + 2].astype(f32)
    group_pos = (place[:, 0] * 256.0 + place[:, 1]).astype(jnp.int32)

    pieces = jnp.concatenate(
        [
            qkv_weight.reshape(part_rows, 3, inner, share)
            .transpose(2, 0, 1, 3)
            .reshape(inner, part_rows, 3 * share),
            fc_in_weight.reshape(part_rows, outer, inner, unit)
            .transpose(2, 0, 1, 3)
            .reshape(inner, part_rows, hidden),
        ],
        axis=2,
    )
    pieces = lax.all_to_all(pieces, "r", 0, 0)
    pieces = lax.all_gather(pieces, "g", axis=0).reshape(width, 3 * share + hidden)
    w_qkv = pieces[:, : 3 * share]
    w_in = pieces[:, 3 * share :]
    w_out = lax.all_gather(fc_out_weight, "g", axis=0, tiled=True)

    vectors = [ln1_gain, ln1_bias, ln2_gain, ln2_bias, dense_bias, fc_out_bias, qkv_bias, fc_in_bias]
    sizes = [v.shape[0] for v in vectors]
    flat = jnp.concatenate(vectors)
    extra = -(-flat.shape[0] // width)
    flat = jnp.pad(flat, (0, extra * width - flat.shape[0])).reshape(extra, width)
    mixed = lax.all_gather(jnp.concatenate([dense_weight, flat], axis=0), ("g", "r"), axis=0)
    w_dense = mixed[:, :part_rows].reshape(width, width)
    w_dense = lax.dynamic_slice_in_dim(w_dense, rank * share, share, axis=0)
    flat = mixed[:, part_rows:].reshape(count, extra * width)
    full = []
    start = 0
    for size in sizes:
        full.append(flat[:, start : start + size].reshape(count * size).astype(f32))
        start += size
    gain_one, shift_one, gain_two, shift_two, bias_dense, bias_out, bias_qkv, bias_in = full
    bias_qkv = lax.dynamic_index_in_dim(bias_qkv.reshape(3, inner, share), rank, 1, False).reshape(-1)
    bias_in = lax.dynamic_index_in_dim(bias_in.reshape(outer, inner, unit), rank, 1, False).reshape(-1)

    normed, _ = norm_stats(group_in)
    left_attn = (normed * gain_one + shift_one).astype(bf)
    left_mlp = (normed * gain_two + shift_two).astype(bf)

    mixed_qkv = jnp.dot(left_attn, w_qkv, preferred_element_type=f32) + bias_qkv
    tables = rotary_tables(group_pos, 2 * share)
    rotated = rotate(mixed_qkv[:, : 2 * share], tables, 1.0).astype(bf)
    queries = rotated[:, :share]
    kv_own = jnp.concatenate([rotated[:, share:], mixed_qkv[:, 2 * share :].astype(bf)], axis=1)
    onward = [(i, i + 1) for i in range(outer - 1)]
    halo = lax.ppermute(kv_own[rows - REACH :], "g", onward)

    pre_act = jnp.dot(left_mlp, w_in, preferred_element_type=f32) + bias_in
    activated, gelu_slope = gelu_pair(pre_act)
    activated_b = activated.astype(bf)
    mlp_out = jnp.dot(activated_b, w_out, preferred_element_type=f32)
    grad_pre = times_transpose(group_top, w_out) * gelu_slope
    grad_pre_b = grad_pre.astype(bf)
    g_out_w = row_sum_product(activated_b, group_top).astype(bf)
    g_in_w = row_sum_product(left_mlp, grad_pre_b).astype(bf)
    g_in_b = jnp.sum(grad_pre, axis=0)
    grad_left_mlp = times_transpose(grad_pre_b, w_in)
    g_out_w = lax.psum_scatter(g_out_w, "g", scatter_dimension=0, tiled=True).astype(f32)
    g_in_w = lax.psum_scatter(g_in_w, "g", scatter_dimension=0, tiled=True)
    g_in_w = lax.all_to_all(g_in_w.reshape(inner, part_rows, hidden), "r", 0, 0)
    g_in_w = (
        g_in_w.reshape(inner, part_rows, outer, unit)
        .transpose(1, 2, 0, 3)
        .reshape(part_rows, count * unit)
        .astype(f32)
    )

    size = BLOCK
    blocks = rows // size
    span = size + REACH
    reach = jnp.concatenate([halo, kv_own], axis=0)
    q_blocks = windows(queries, blocks, size, size)
    k_blocks = windows(reach[:, :share], blocks, size, span)
    v_blocks = windows(reach[:, share:], blocks, size, span)
    spread = jnp.arange(size, dtype=jnp.int32)[:, None] + REACH - jnp.arange(span, dtype=jnp.int32)[None]
    allowed = (spread >= 0)[None] & (spread[None] <= group_pos.reshape(blocks, size, 1))
    scores = jnp.einsum("nhqd,nhkd->nhqk", q_blocks, k_blocks, preferred_element_type=f32) * HD ** (-0.5)
    scores = jnp.where(allowed[:, None], scores, -jnp.inf)
    row_max = jnp.max(scores, axis=-1, keepdims=True)
    exp_total = jnp.sum(jnp.exp(scores - row_max), axis=-1, keepdims=True)
    probs = jnp.exp(scores - (row_max + jnp.log(exp_total)))
    probs_b = probs.astype(bf)
    context = jnp.einsum("nhqk,nhkd->nhqd", probs_b, v_blocks, preferred_element_type=f32)
    context_b = context.astype(bf).transpose(0, 2, 1, 3).reshape(rows, share)
    attn_out = jnp.dot(context_b, w_dense, preferred_element_type=f32)
    out_part = (attn_out + mlp_out).astype(bf)
    out_sum = lax.psum_scatter(out_part, "r", scatter_dimension=0, tiled=True).astype(f32)
    result = (layer_input.astype(f32) + out_sum + (bias_dense + bias_out)).astype(bf)

    g_dense_w = row_sum_product(context_b, group_top).astype(bf)
    g_dense_w = lax.dynamic_update_slice_in_dim(
        jnp.zeros((width, width), bf), g_dense_w, rank * share, axis=0
    )
    g_dense_w = lax.psum_scatter(g_dense_w, ("g", "r"), scatter_dimension=0, tiled=True).astype(f32)
    grad_context = times_transpose(group_top, w_dense).astype(bf)
    c_blocks = windows(grad_context, blocks, size, size)
    grad_probs = jnp.einsum("nhqd,nhkd->nhqk", c_blocks, v_blocks, preferred_element_type=f32)
    row_dot = jnp.sum(probs * grad_probs, axis=-1, keepdims=True)
    grad_scores = (probs * (grad_probs - row_dot) * HD ** (-0.5)).astype(bf)
    g_q = jnp.einsum("nhqk,nhkd->nhqd", grad_scores, k_blocks, preferred_element_type=f32)
    g_k = jnp.einsum("nhqk,nhqd->nhkd", grad_scores, q_blocks, preferred_element_type=f32)
    g_v = jnp.einsum("nhqk,nhqd->nhkd", probs_b, c_blocks, preferred_element_type=f32)
    g_q = g_q.transpose(0, 2, 1, 3).reshape(rows, share)
    g_kv = jnp.concatenate(
        [unwindow(g_k, blocks, size, span), unwindow(g_v, blocks, size, span)], axis=1
    )
    back = [(i + 1, i) for i in range(outer - 1)]
    returned = lax.ppermute(g_kv[:REACH].astype(bf), "g", back).astype(f32)
    g_kv = g_kv[REACH:] + jnp.pad(returned, ((rows - REACH, 0), (0, 0)))
    g_qk = rotate(jnp.concatenate([g_q, g_kv[:, :share]], axis=1), tables, -1.0)
    grad_qkv = jnp.concatenate([g_qk, g_kv[:, share:]], axis=1)
    grad_qkv_b = grad_qkv.astype(bf)
    g_qkv_w = row_sum_product(left_attn, grad_qkv_b)
    g_qkv_b = jnp.sum(grad_qkv, axis=0)
    grad_left_attn = times_transpose(grad_qkv_b, w_qkv)

    grad_normed = (grad_left_attn * gain_one + grad_left_mlp * gain_two).astype(bf)
    grad_normed = lax.psum_scatter(grad_normed, "r", scatter_dimension=0, tiled=True).astype(f32)

    mine = (jnp.arange(inner) == rank).astype(f32)
    top_f = cotangent.astype(f32)
    sums = [
        jnp.sum(grad_left_attn * normed, axis=0),
        jnp.sum(grad_left_attn, axis=0),
        jnp.sum(grad_left_mlp * normed, axis=0),
        jnp.sum(grad_left_mlp, axis=0),
        jnp.sum(top_f, axis=0),
        (g_qkv_b.reshape(3, 1, share) * mine[None, :, None]).reshape(-1),
        (g_in_b.reshape(outer, 1, unit) * mine[None, :, None]).reshape(-1),
    ]
    lengths = [s.shape[0] // count for s in sums]
    columns = sum(lengths) // part_rows
    table = jnp.concatenate([s.reshape(count, -1) for s in sums], axis=1)
    table = table.reshape(count, columns, part_rows).transpose(0, 2, 1).reshape(width, columns)
    table = jnp.pad(table, ((0, 0), (0, 128 - columns)))
    last = jnp.concatenate([g_qkv_w, table], axis=1).astype(bf)
    last = lax.psum_scatter(last, "g", scatter_dimension=0, tiled=True)
    last = lax.all_to_all(last.reshape(inner, part_rows, 3 * share + 128), "r", 0, 0).astype(f32)
    g_qkv_w = (
        last[:, :, : 3 * share]
        .reshape(inner, part_rows, 3, share)
        .transpose(1, 2, 0, 3)
        .reshape(part_rows, 3 * width)
    )
    table = jnp.sum(last[:, :, 3 * share : 3 * share + columns], axis=0)
    table = table.transpose(1, 0).reshape(-1)
    out = []
    start = 0
    for length in lengths:
        out.append(table[start : start + length])
        start += length

    own_normed, inv_scale = norm_stats(layer_input)
    grad_in = top_f + inv_scale * (
        grad_normed
        - jnp.mean(grad_normed, axis=-1, keepdims=True)
        - own_normed * jnp.mean(grad_normed * own_normed, axis=-1, keepdims=True)
    )
    return (
        result,
        grad_in,
        out[0],
        out[1],
        g_qkv_w,
        out[5],
        g_dense_w,
        out[4],
        out[2],
        out[3],
        g_in_w,
        out[6],
        g_out_w,
        out[4],
    )


def solution(mesh):
    inner = GROUP
    split = Mesh(mesh.devices.reshape(-1, inner), ("g", "r"))
    flat = P(("g", "r"))
    tall = P(("g", "r"), None)
    in_specs = (
        tall, flat, flat, tall, flat, tall, flat, flat, flat, tall, flat, tall, flat, flat, tall,
    )
    out_specs = (
        tall, tall, flat, flat, tall, flat, tall, flat, flat, flat, tall, flat, tall, flat,
    )
    return jax.shard_map(body, mesh=split, in_specs=in_specs, out_specs=out_specs, check_vma=False)
```

```python
import jax
import jax.numpy as jnp
from jax import lax
from jax.sharding import Mesh
from jax.sharding import PartitionSpec as P

HEADS = 16
HD = 64
ROT = 16
REACH = 512
GROUP = 8
BLOCK = 256


EPSILON = 1e-05
ROPE_BASE = 10000.0


def norm_stats(inputs):
    values_f = inputs.astype(jnp.float32)
    centre = jnp.mean(values_f, axis=-1, keepdims=True)
    shifted = values_f - centre
    variance = jnp.mean(shifted * shifted, axis=-1, keepdims=True)
    inv_scale = lax.rsqrt(variance + EPSILON)
    return (shifted * inv_scale, inv_scale)


def rotary_tables(positions, lanes):
    place = jnp.arange(lanes, dtype=jnp.int32) % HD
    counter = (place % (ROT // 2)).astype(jnp.float32)
    frequency = ROPE_BASE ** (-2.0 * counter / ROT)
    frequency = jnp.where(place < ROT, frequency, 0.0)
    angles = positions.astype(jnp.float32)[:, None] * frequency[None, :]
    sine = jnp.sin(angles)
    lower = jnp.where(place < ROT // 2, -sine, 0.0)
    upper = jnp.where(place >= ROT // 2, sine, 0.0)
    return (jnp.cos(angles), lower, upper)


def rotate(rows, tables, orient):
    cosine, lower, upper = tables
    ahead = jnp.roll(rows, -(ROT // 2), axis=1)
    behind = jnp.roll(rows, ROT // 2, axis=1)
    return rows * cosine + orient * (ahead * lower + behind * upper)


def windows(rows, blocks, size, span):
    heads = rows.shape[1] // HD
    cut = jnp.stack([rows[i * size : i * size + span] for i in range(blocks)])
    return cut.reshape(blocks, span, heads, HD).transpose(0, 2, 1, 3)


def unwindow(grads, blocks, size, span):
    parts = span // size
    heads = grads.shape[1]
    rows = grads.transpose(0, 2, 1, 3).reshape(blocks, parts, size, heads * HD)
    total = None
    for part in range(parts):
        piece = jnp.pad(rows[:, part], ((part, parts - 1 - part), (0, 0), (0, 0)))
        total = piece if total is None else total + piece
    return total.reshape((blocks + parts - 1) * size, heads * HD)


def gelu_pair(pre_act):
    cumulative = 0.5 * (1.0 + lax.erf(pre_act * 0.7071067811865476))
    density = jnp.exp(-0.5 * pre_act * pre_act) * 0.3989422804014327
    return (pre_act * cumulative, cumulative + pre_act * density)


def row_sum_product(left_side, right_side):
    return lax.dot_general(
        left_side, right_side, (((0,), (0,)), ((), ())), preferred_element_type=jnp.float32
    )


def times_transpose(left_side, right_side):
    return lax.dot_general(
        left_side, right_side, (((1,), (1,)), ((), ())), preferred_element_type=jnp.float32
    )


def body(
    layer_input,
    ln1_gain,
    ln1_bias,
    qkv_weight,
    qkv_bias,
    dense_weight,
    dense_bias,
    ln2_gain,
    ln2_bias,
    fc_in_weight,
    fc_in_bias,
    fc_out_weight,
    fc_out_bias,
    positions,
    cotangent,
):
    bf = jnp.bfloat16
    f32 = jnp.float32
    outer = lax.axis_size("g")
    inner = lax.axis_size("r")
    count = outer * inner
    rank = lax.axis_index("r")
    tok_rows, width = layer_input.shape
    part_rows = qkv_weight.shape[0]
    share = width // inner
    unit = fc_out_weight.shape[0]
    hidden = outer * unit
    rows = inner * tok_rows

    place = jnp.stack([positions // 256, positions % 256], axis=1).astype(bf)
    place = jnp.pad(place, ((0, 0), (0, 126)))
    tokens = jnp.concatenate([layer_input, cotangent, place], axis=1)
    tokens = lax.all_gather(tokens, "r", axis=0, tiled=True)
    group_in = tokens[:, :width]
    group_top = tokens[:, width : 2 * width]
    place = tokens[:, 2 * width : 2 * width + 2].astype(f32)
    group_pos = (place[:, 0] * 256.0 + place[:, 1]).astype(jnp.int32)

    pieces = jnp.concatenate(
        [
            qkv_weight.reshape(part_rows, 3, inner, share)
            .transpose(2, 0, 1, 3)
            .reshape(inner, part_rows, 3 * share),
            fc_in_weight.reshape(part_rows, outer, inner, unit)
            .transpose(2, 0, 1, 3)
            .reshape(inner, part_rows, hidden),
        ],
        axis=2,
    )
    pieces = lax.all_to_all(pieces, "r", 0, 0)
    pieces = lax.all_gather(pieces, "g", axis=0).reshape(width, 3 * share + hidden)
    w_qkv = pieces[:, : 3 * share]
    w_in = pieces[:, 3 * share :]
    w_out = lax.all_gather(fc_out_weight, "g", axis=0, tiled=True)

    vectors = [ln1_gain, ln1_bias, ln2_gain, ln2_bias, dense_bias, fc_out_bias, qkv_bias, fc_in_bias]
    sizes = [v.shape[0] for v in vectors]
    flat = jnp.concatenate(vectors)
    extra = -(-flat.shape[0] // width)
    flat = jnp.pad(flat, (0, extra * width - flat.shape[0])).reshape(extra, width)
    mixed = lax.all_gather(jnp.concatenate([dense_weight, flat], axis=0), ("g", "r"), axis=0)
    w_dense = mixed[:, :part_rows].reshape(width, width)
    w_dense = lax.dynamic_slice_in_dim(w_dense, rank * share, share, axis=0)
    flat = mixed[:, part_rows:].reshape(count, extra * width)
    full = []
    start = 0
    for size in sizes:
        full.append(flat[:, start : start + size].reshape(count * size).astype(f32))
        start += size
    gain_one, shift_one, gain_two, shift_two, bias_dense, bias_out, bias_qkv, bias_in = full
    bias_qkv = lax.dynamic_index_in_dim(bias_qkv.reshape(3, inner, share), rank, 1, False).reshape(-1)
    bias_in = lax.dynamic_index_in_dim(bias_in.reshape(outer, inner, unit), rank, 1, False).reshape(-1)

    normed, _ = norm_stats(group_in)
    left_attn = (normed * gain_one + shift_one).astype(bf)
    left_mlp = (normed * gain_two + shift_two).astype(bf)

    mixed_qkv = jnp.dot(left_attn, w_qkv, preferred_element_type=f32) + bias_qkv
    tables = rotary_tables(group_pos, 2 * share)
    rotated = rotate(mixed_qkv[:, : 2 * share], tables, 1.0).astype(bf)
    queries = rotated[:, :share]
    kv_own = jnp.concatenate([rotated[:, share:], mixed_qkv[:, 2 * share :].astype(bf)], axis=1)
    onward = [(i, i + 1) for i in range(outer - 1)]
    halo = lax.ppermute(kv_own[rows - REACH :], "g", onward)

    pre_act = jnp.dot(left_mlp, w_in, preferred_element_type=f32) + bias_in
    activated, gelu_slope = gelu_pair(pre_act)
    activated_b = activated.astype(bf)
    mlp_out = jnp.dot(activated_b, w_out, preferred_element_type=f32)
    grad_pre = times_transpose(group_top, w_out) * gelu_slope
    grad_pre_b = grad_pre.astype(bf)
    g_out_w = row_sum_product(activated_b, group_top).astype(bf)
    g_in_w = row_sum_product(left_mlp, grad_pre_b).astype(bf)
    g_in_b = jnp.sum(grad_pre, axis=0)
    grad_left_mlp = times_transpose(grad_pre_b, w_in)
    g_out_w = lax.psum_scatter(g_out_w, "g", scatter_dimension=0, tiled=True).astype(f32)
    g_in_w = lax.psum_scatter(g_in_w, "g", scatter_dimension=0, tiled=True)
    g_in_w = lax.all_to_all(g_in_w.reshape(inner, part_rows, hidden), "r", 0, 0)
    g_in_w = (
        g_in_w.reshape(inner, part_rows, outer, unit)
        .transpose(1, 2, 0, 3)
        .reshape(part_rows, count * unit)
        .astype(f32)
    )

    size = BLOCK
    blocks = rows // size
    span = size + REACH
    reach = jnp.concatenate([halo, kv_own], axis=0)
    q_blocks = windows(queries, blocks, size, size)
    k_blocks = windows(reach[:, :share], blocks, size, span)
    v_blocks = windows(reach[:, share:], blocks, size, span)
    spread = jnp.arange(size, dtype=jnp.int32)[:, None] + REACH - jnp.arange(span, dtype=jnp.int32)[None]
    allowed = (spread >= 0)[None] & (spread[None] <= group_pos.reshape(blocks, size, 1))
    scores = jnp.einsum("nhqd,nhkd->nhqk", q_blocks, k_blocks, preferred_element_type=f32) * HD ** (-0.5)
    scores = jnp.where(allowed[:, None], scores, -jnp.inf)
    row_max = jnp.max(scores, axis=-1, keepdims=True)
    exp_total = jnp.sum(jnp.exp(scores - row_max), axis=-1, keepdims=True)
    probs = jnp.exp(scores - (row_max + jnp.log(exp_total)))
    probs_b = probs.astype(bf)
    context = jnp.einsum("nhqk,nhkd->nhqd", probs_b, v_blocks, preferred_element_type=f32)
    context_b = context.astype(bf).transpose(0, 2, 1, 3).reshape(rows, share)
    attn_out = jnp.dot(context_b, w_dense, preferred_element_type=f32)
    out_part = (attn_out + mlp_out).astype(bf)
    out_sum = lax.psum_scatter(out_part, "r", scatter_dimension=0, tiled=True).astype(f32)
    result = (layer_input.astype(f32) + out_sum + (bias_dense + bias_out)).astype(bf)

    g_dense_w = row_sum_product(context_b, group_top).astype(bf)
    g_dense_w = lax.psum_scatter(g_dense_w, "g", scatter_dimension=1, tiled=True)
    stripe = g_dense_w.shape[1]
    g_dense_w = lax.dynamic_update_slice_in_dim(
        jnp.zeros((width, stripe), bf), g_dense_w, rank * share, axis=0
    )
    g_dense_w = lax.all_to_all(
        g_dense_w.reshape(count, part_rows, stripe), ("g", "r"), 0, 0
    )
    g_dense_w = g_dense_w.reshape(outer, inner, part_rows, stripe).astype(f32).sum(axis=1)
    g_dense_w = g_dense_w.transpose(1, 0, 2).reshape(part_rows, width)
    grad_context = times_transpose(group_top, w_dense).astype(bf)
    c_blocks = windows(grad_context, blocks, size, size)
    grad_probs = jnp.einsum("nhqd,nhkd->nhqk", c_blocks, v_blocks, preferred_element_type=f32)
    row_dot = jnp.sum(probs * grad_probs, axis=-1, keepdims=True)
    grad_scores = (probs * (grad_probs - row_dot) * HD ** (-0.5)).astype(bf)
    g_q = jnp.einsum("nhqk,nhkd->nhqd", grad_scores, k_blocks, preferred_element_type=f32)
    g_k = jnp.einsum("nhqk,nhqd->nhkd", grad_scores, q_blocks, preferred_element_type=f32)
    g_v = jnp.einsum("nhqk,nhqd->nhkd", probs_b, c_blocks, preferred_element_type=f32)
    g_q = g_q.transpose(0, 2, 1, 3).reshape(rows, share)
    g_kv = jnp.concatenate(
        [unwindow(g_k, blocks, size, span), unwindow(g_v, blocks, size, span)], axis=1
    )
    back = [(i + 1, i) for i in range(outer - 1)]
    returned = lax.ppermute(g_kv[:REACH].astype(bf), "g", back).astype(f32)
    g_kv = g_kv[REACH:] + jnp.pad(returned, ((rows - REACH, 0), (0, 0)))
    g_qk = rotate(jnp.concatenate([g_q, g_kv[:, :share]], axis=1), tables, -1.0)
    grad_qkv = jnp.concatenate([g_qk, g_kv[:, share:]], axis=1)
    grad_qkv_b = grad_qkv.astype(bf)
    g_qkv_w = row_sum_product(left_attn, grad_qkv_b)
    g_qkv_b = jnp.sum(grad_qkv, axis=0)
    grad_left_attn = times_transpose(grad_qkv_b, w_qkv)

    grad_normed = (grad_left_attn * gain_one + grad_left_mlp * gain_two).astype(bf)
    grad_normed = lax.psum_scatter(grad_normed, "r", scatter_dimension=0, tiled=True).astype(f32)

    mine = (jnp.arange(inner) == rank).astype(f32)
    top_f = cotangent.astype(f32)
    sums = [
        jnp.sum(grad_left_attn * normed, axis=0),
        jnp.sum(grad_left_attn, axis=0),
        jnp.sum(grad_left_mlp * normed, axis=0),
        jnp.sum(grad_left_mlp, axis=0),
        jnp.sum(top_f, axis=0),
        (g_qkv_b.reshape(3, 1, share) * mine[None, :, None]).reshape(-1),
        (g_in_b.reshape(outer, 1, unit) * mine[None, :, None]).reshape(-1),
    ]
    lengths = [s.shape[0] // count for s in sums]
    columns = sum(lengths) // part_rows
    table = jnp.concatenate([s.reshape(count, -1) for s in sums], axis=1)
    table = table.reshape(count, columns, part_rows).transpose(0, 2, 1).reshape(width, columns)
    table = jnp.pad(table, ((0, 0), (0, 128 - columns)))
    last = jnp.concatenate([g_qkv_w, table], axis=1).astype(bf)
    last = lax.psum_scatter(last, "g", scatter_dimension=0, tiled=True)
    last = lax.all_to_all(last.reshape(inner, part_rows, 3 * share + 128), "r", 0, 0).astype(f32)
    g_qkv_w = (
        last[:, :, : 3 * share]
        .reshape(inner, part_rows, 3, share)
        .transpose(1, 2, 0, 3)
        .reshape(part_rows, 3 * width)
    )
    table = jnp.sum(last[:, :, 3 * share : 3 * share + columns], axis=0)
    table = table.transpose(1, 0).reshape(-1)
    out = []
    start = 0
    for length in lengths:
        out.append(table[start : start + length])
        start += length

    own_normed, inv_scale = norm_stats(layer_input)
    grad_in = top_f + inv_scale * (
        grad_normed
        - jnp.mean(grad_normed, axis=-1, keepdims=True)
        - own_normed * jnp.mean(grad_normed * own_normed, axis=-1, keepdims=True)
    )
    return (
        result,
        grad_in,
        out[0],
        out[1],
        g_qkv_w,
        out[5],
        g_dense_w,
        out[4],
        out[2],
        out[3],
        g_in_w,
        out[6],
        g_out_w,
        out[4],
    )


def solution(mesh):
    inner = GROUP
    split = Mesh(mesh.devices.reshape(-1, inner), ("g", "r"))
    flat = P(("g", "r"))
    tall = P(("g", "r"), None)
    in_specs = (
        tall, flat, flat, tall, flat, tall, flat, flat, flat, tall, flat, tall, flat, flat, tall,
    )
    out_specs = (
        tall, tall, flat, flat, tall, flat, tall, flat, flat, flat, tall, flat, tall, flat,
    )
    return jax.shard_map(body, mesh=split, in_specs=in_specs, out_specs=out_specs, check_vma=False)
```
